256 devices in a mesh: band: 8 (over x, core), col: 32 (over z, y).
Axes of the slice: x: 4, y: 4, z: 8, core: 2. Of those that a mesh axis runs over, the one named last changes fastest.
Arguments:
- fields_in: float32 [6, 137, 32, 4096], P(None, None, 'band', 'col'), may hold values from -6 to 6
- drag_rate: float32 [137], replicated, may hold values from 0.1 to 1
- loss_rate: float32 [4, 137], replicated, may hold values from 0.1 to 1
- diffusivity: float32 [6, 136], replicated, may hold values from 0.1 to 10
- owner_col: int32 [8, 16384, 1], P('band', 'col'), may hold values from 0 to 31; in each aligned block of 512 rows (0 to 511, 512 to 1023, ..., all dimensions but the last counted through in order) at most 32 rows name the same one
- anchor_cell: int32 [8, 16384], P('band', 'col'), may hold values from 0 to 124
- offsets: float32 [2, 8, 16384], P(None, 'band', 'col'), may hold values from 0 to 1
- stencil: float32 [4, 32, 4096], P(None, 'band', 'col'), may hold values from 0.02 to 0.24
Outputs:
- fields_out: float32 [6, 137, 32, 4096], P(None, None, 'band', 'col')
The draws below stay inside these ranges and needn't reach their ends.
Inputs may be any that keep to these rules, and one draw needn't show every extreme that they name: `owner_col`: among the columns of one device at most 32 have the same owner; on some device one owner has exactly 32 of them. The stencil lies inside the owner's block: row anchor_cell // 125, longitude anchor_cell % 125.
All inputs are finite; a program needn't handle non-finite values.
Results may differ from the reference program's by a relative error of at most 0.00002.
Values sent between devices are 32-bit elements; how exact they have to be, the bound alone decides.
No kernel may reach another device: no remote copies, remote signals or barrier semaphores. Data moves between devices by JAX's collectives and lax.ppermute only.
A program may use at most 128 MiB of HBM per device.

```python
import math
import jax
import jax.numpy as jnp
import numpy as np
from jax import lax

LEV = 137
TRACERS = 4
FIELDS = 6
PLAT = 4
PLON = 128
COLS = 512
CAP = 32
NLAT = 32
NLON = 4096
N_BAND = 8
N_COL = 32


def plant(drawn, stream_key, least, high):
    dims = drawn.shape
    spot = [jax.random.randint(jax.random.fold_in(stream_key, axis), (), 0, dims[axis]) for axis in range(len(dims))]
    drawn = drawn.at[tuple(spot)].set(least)
    longest = dims.index(max(dims))
    spot[longest] = (spot[longest] + 1) % dims[longest]
    return drawn.at[tuple(spot)].set(high)


def level_of(stream_key, extent, split, least, top_value):
    def one(axis_at, blocks):
        heights = jax.random.uniform(jax.random.fold_in(jax.random.fold_in(stream_key, 6), axis_at), (blocks,), jnp.float32, least / len(split), top_value / len(split))
        return jnp.repeat(jnp.exp(heights), extent[axis_at] // blocks).reshape((-1,) + (1,) * (len(extent) - axis_at - 1))

    factor_of = one(*split[0])
    for cut in split[1:]:
        factor_of = factor_of * one(*cut)
    return factor_of


def deal_out(stream_key, own, number, rows, number_of, top, bound, lean):
    sequence = jax.random.permutation(stream_key, number_of)
    packed, usual = load_shares(number_of, rows * top, bound, lean, True), load_shares(number_of, rows * top, bound, lean, False)
    places = jnp.arange(number_of)

    def named(sizes, offset_by):
        used = int((sizes > 0).sum())
        fixed = max(1, used // 4)
        passed = fixed + (places - fixed + offset_by * (used - fixed)) % max(1, number_of - fixed)
        return jnp.zeros((number_of,), jnp.int32).at[sequence[jnp.where(places < fixed, places, passed)]].set(jnp.asarray(sizes, jnp.int32))

    sizes = jnp.where(number % 4 == 0, named(packed, number // 4), named(usual, number - number // 4 - 1))
    mixed = jax.random.permutation(jax.random.fold_in(own, 3), number_of)
    donor, receiver = mixed[0:number_of // 2 * 2:2], mixed[1:number_of // 2 * 2:2]
    margin = jnp.minimum(sizes[donor] - 1, bound - sizes[receiver]) // 2
    margin = jnp.where((donor == sequence[0]) | (receiver == sequence[0]) | (sizes[receiver] == 0), 0, jnp.maximum(margin, 0))
    passed = jax.random.randint(jax.random.fold_in(own, 4), (number_of // 2,), 0, 1 << 20) % (margin + 1)
    sizes = sizes.at[donor].add(-passed).at[receiver].add(passed)
    labels = jnp.searchsorted(jnp.cumsum(sizes), jnp.arange(rows * top), side="right").astype(jnp.int32)
    table = labels.reshape(top, rows).T
    table = table[jax.random.permutation(jax.random.fold_in(own, 1), rows)]
    offset_by = jax.random.randint(jax.random.fold_in(own, 2), (rows, 1), 0, top)
    return jnp.take_along_axis(table, (jnp.arange(top)[None, :] + offset_by) % top, axis=1)


def load_shares(number_of, total, limit, skew, full):
    portions = [(1 << 20) // math.isqrt(standing ** skew) + 1 for standing in range(1, number_of + 1)]
    largest = limit if full else min(limit, max(-(-total // number_of), total * portions[0] // sum(portions)))
    least = 1 if total - largest >= number_of - 1 else 0
    holding, surplus = [largest] + [least] * (number_of - 1), total - largest - least * (number_of - 1)
    while surplus > 0:
        candidates = [i for i in range(1, number_of) if holding[i] < largest] or [i for i in range(1, number_of) if holding[i] < limit]
        mass, remaining = sum([portions[i] for i in candidates]), surplus
        for i in candidates:
            more = min(limit - holding[i], max(1, remaining * portions[i] // mass), surplus)
            holding[i] = holding[i] + more
            surplus = surplus - more
    return np.array(holding)


def bell_draw(key, extent, width, reach, cuts=(), held_as=jnp.bfloat16):
    values = jax.random.normal(key, extent, jnp.float32) * width
    if len(cuts) > 0:
        values = level_of(key, extent, cuts, -0.22, 0.18) * values
    return jnp.clip(values, min=-reach, max=reach).astype(held_as)


def setup_inputs(seed: int = 0) -> dict:
    keys = jax.random.split(jax.random.key(seed), 9)
    fields_in = bell_draw(keys[0], (FIELDS, LEV, NLAT, NLON), 1.0, 6.0, ((2, 8), (3, 32)), jnp.float32)
    drag_rate = jnp.clip(jnp.exp(jax.random.uniform(keys[1], (LEV,), jnp.float32, math.log(0.1), math.log(1.0))), 0.1, 1.0)
    loss_rate = jnp.clip(jnp.exp(jax.random.uniform(keys[2], (TRACERS, LEV), jnp.float32, math.log(0.1), math.log(1.0))), 0.1, 1.0)
    diffusivity = jnp.clip(jnp.exp(jax.random.uniform(keys[3], (FIELDS, LEV - 1), jnp.float32, math.log(0.1), math.log(10.0))), 0.1, 10.0)
    owner_col_keys = jax.random.split(jax.random.fold_in(keys[4], 1), N_BAND * (N_COL * COLS) // COLS)
    owner_col_turns = jax.random.permutation(jax.random.fold_in(keys[4], 3), N_BAND * (N_COL * COLS) // COLS)
    owner_col = jax.vmap(lambda own, number: deal_out(jax.random.fold_in(keys[4], 2), own, number, COLS, N_COL, 1, CAP, 2))(owner_col_keys, owner_col_turns).reshape((N_BAND, N_COL * COLS, 1))
    anchor_cell = plant(jax.random.randint(keys[5], (N_BAND, N_COL * COLS), 0, (PLAT - 3) * (PLON - 3)), jax.random.fold_in(keys[5], 1), 0, ((PLAT - 3) * (PLON - 3)) - 1).astype(jnp.int32)
    offsets = jnp.clip(1.0 * jax.random.uniform(keys[6], (2, N_BAND, N_COL * COLS), jnp.float32) ** level_of(keys[6], (2, N_BAND, N_COL * COLS), ((1, 8), (2, 32)), -0.2, 0.2), 0.0, 1.0)
    stencil = jnp.clip(jnp.exp(math.log(0.24) - 2.4849066 * jax.random.uniform(keys[7], (4, NLAT, NLON), jnp.float32) ** level_of(keys[7], (4, NLAT, NLON), ((1, 8), (2, 32)), -0.2, 0.2)), 0.02, 0.24)
    return {"fields_in": fields_in, "drag_rate": drag_rate, "loss_rate": loss_rate, "diffusivity": diffusivity, "owner_col": owner_col, "anchor_cell": anchor_cell, "offsets": offsets, "stencil": stencil}


def cubic_weights(frac):
    return (-frac * (frac - 1.0) * (frac - 2.0) / 6.0, (frac + 1.0) * (frac - 1.0) * (frac - 2.0) / 2.0, -(frac + 1.0) * frac * (frac - 2.0) / 2.0, (frac + 1.0) * frac * (frac - 1.0) / 6.0)

def interp_rows(pick_cells, frac_lon):
    lon_weights = cubic_weights(frac_lon)
    edge_low = (1.0 - frac_lon) * pick_cells(0, 1) + frac_lon * pick_cells(0, 2)
    inner_low = lon_weights[0] * pick_cells(1, 0) + lon_weights[1] * pick_cells(1, 1) + lon_weights[2] * pick_cells(1, 2) + lon_weights[3] * pick_cells(1, 3)
    inner_high = lon_weights[0] * pick_cells(2, 0) + lon_weights[1] * pick_cells(2, 1) + lon_weights[2] * pick_cells(2, 2) + lon_weights[3] * pick_cells(2, 3)
    edge_high = (1.0 - frac_lon) * pick_cells(3, 1) + frac_lon * pick_cells(3, 2)
    return (edge_low, inner_low, inner_high, edge_high)

def combine_rows(row_values, frac_lat):
    lat_weights = cubic_weights(frac_lat)
    return lat_weights[0] * row_values[0] + lat_weights[1] * row_values[1] + lat_weights[2] * row_values[2] + lat_weights[3] * row_values[3]

def tendency(fields_in, drag_rate, loss_rate):
    wind_speed = jnp.sqrt(fields_in[0] * fields_in[0] + fields_in[1] * fields_in[1] + 1.0)
    wind_part = -drag_rate[:, None, None] * wind_speed * fields_in[:2]
    tracer_part = -loss_rate[:, :, None, None] * fields_in[2:]
    return 0.5 * jnp.concatenate([wind_part, tracer_part], axis=0)

def vertical(field, diffusivity):
    levels = field.shape[1]
    lower_side = jnp.transpose(jnp.pad(diffusivity, ((0, 0), (1, 0))))
    upper_side = jnp.transpose(jnp.pad(diffusivity, ((0, 0), (0, 1))))

    def eliminate(prev_ratio, coeffs):
        low_coef, up_coef = coeffs
        denom = 1.0 + low_coef + up_coef - low_coef * prev_ratio
        ratio = up_coef / denom
        return (ratio, (denom, ratio))
    _, (denoms, ratios) = lax.scan(eliminate, jnp.zeros_like(lower_side[0]), (lower_side, upper_side))

    def forward(level, state):
        previous, buffer = state
        row_now = lax.dynamic_index_in_dim(field, level, 1, keepdims=False)
        fresh = (row_now + lower_side[level][:, None] * previous) / denoms[level][:, None]
        return (fresh, lax.dynamic_update_index_in_dim(buffer, fresh, level, 1))
    last_row, reduced = lax.fori_loop(0, levels, forward, (jnp.zeros_like(field[:, 0]), jnp.zeros_like(field)))

    def backward(step, state):
        level = levels - 2 - step
        following, buffer = state
        row_now = lax.dynamic_index_in_dim(buffer, level, 1, keepdims=False)
        fresh = row_now + ratios[level][:, None] * following
        return (fresh, lax.dynamic_update_index_in_dim(buffer, fresh, level, 1))
    _, solved = lax.fori_loop(0, levels - 1, backward, (last_row, reduced))
    return solved

def apply_stencil(padded, field, stencil):
    from_north = padded[:, :, :-2, 1:-1]
    from_south = padded[:, :, 2:, 1:-1]
    from_west = padded[:, :, 1:-1, :-2]
    from_east = padded[:, :, 1:-1, 2:]
    return field + stencil[0] * (from_north - field) + stencil[1] * (from_south - field) + stencil[2] * (from_west - field) + stencil[3] * (from_east - field)

def to_grid(blocked):
    fields = blocked.shape[0]
    shaped = blocked.reshape(fields, LEV, N_BAND, N_COL, PLAT, PLON)
    shaped = jnp.transpose(shaped, (0, 1, 2, 4, 3, 5))
    return shaped.reshape(fields, LEV, NLAT, NLON)

def reference(fields_in, drag_rate, loss_rate, diffusivity, owner_col, anchor_cell, offsets, stencil):
    fields = fields_in.shape[0]
    half = tendency(fields_in, drag_rate, loss_rate)
    moved = fields_in + half
    band_rows = (jnp.arange(N_BAND, dtype=jnp.int32) * PLAT)[:, None]
    owners = owner_col[:, :, 0].astype(jnp.int32)
    row_in = anchor_cell // (PLON - 3)
    lon_in = anchor_cell % (PLON - 3)
    base_cell = ((band_rows + row_in) * NLON + owners * PLON + lon_in).reshape(-1).astype(jnp.int32)
    frac_lon = offsets[0].reshape(-1)
    frac_lat = offsets[1].reshape(-1)
    flattened = moved.reshape(fields, LEV, NLAT * NLON)

    def one_field(values):

        def pick_cells(offset_row, offset_lon):
            return jnp.take(values, base_cell + offset_row * NLON + offset_lon, axis=1)
        return combine_rows(interp_rows(pick_cells, frac_lon), frac_lat)
    depart = lax.map(one_field, flattened)
    depart = to_grid(depart.reshape(fields, LEV, N_BAND, N_COL * COLS))
    rhs = depart + half
    solved = vertical(rhs.reshape(fields, LEV, NLAT * NLON), diffusivity).reshape(fields_in.shape)
    padded = jnp.pad(solved, ((0, 0), (0, 0), (1, 1), (1, 1)))
    return apply_stencil(padded, solved, stencil)
```

```python
import jax
import jax.numpy as jnp
from jax import lax
from jax.experimental import pallas as pl
from jax.experimental.pallas import tpu as pltpu
from jax.sharding import PartitionSpec as P

F32 = jnp.float32
BF16 = jnp.bfloat16
HI = lax.Precision.HIGHEST
FIELDS = 6
LEV = 137
ROWS = 4
LON = 128
CELLS = 512
PEERS = 32
CAP = 32
LANES = 128
GROUPS = LANES // CAP
FLAT = FIELDS * LEV
CHUNK = 208
PADDED = GROUPS * CHUNK
LEV_PAD = 256


def iota(shape, dim):
    return lax.broadcasted_iota(jnp.int32, shape, dim)


def dot_nn(a, b, precision=None):
    return lax.dot_general(
        a, b, (((1,), (0,)), ((), ())), precision=precision, preferred_element_type=F32
    )


def dot_nt(a, b, precision=None):
    return lax.dot_general(
        a, b, (((1,), (1,)), ((), ())), precision=precision, preferred_element_type=F32
    )


def cubic_weights(frac):
    return (
        -frac * (frac - 1.0) * (frac - 2.0) / 6.0,
        (frac + 1.0) * (frac - 1.0) * (frac - 2.0) / 2.0,
        -(frac + 1.0) * frac * (frac - 2.0) / 2.0,
        (frac + 1.0) * frac * (frac - 1.0) / 6.0,
    )


def split_2(x):
    high = x.astype(BF16)
    return high, (x - high.astype(F32)).astype(BF16)


def group_transpose(parts):
    group = iota(parts[0].shape, 1) // CAP

    def pick(choices):
        out = choices[0]
        for n in range(1, GROUPS):
            out = jnp.where(group == n, choices[n], out)
        return out

    turned = []
    for shift in range(GROUPS):
        mixed = pick([parts[(n + shift) % GROUPS] for n in range(GROUPS)])
        turned.append(pltpu.roll(mixed, shift * CAP, 1) if shift else mixed)
    return [pick([turned[(n - b) % GROUPS] for n in range(GROUPS)]) for b in range(GROUPS)]


def request_kernel(owner_ref, anchor_ref, offsets_ref, req_ref, slot_ref):
    owner = owner_ref[...]
    onehot = (iota((PEERS, CELLS), 0) == owner).astype(F32)
    earlier = (iota((CELLS, CELLS), 0) < iota((CELLS, CELLS), 1)).astype(BF16)
    before = dot_nn(onehot.astype(BF16), earlier)
    position = jnp.sum(onehot * before, axis=0, keepdims=True).astype(jnp.int32)
    slot_ref[...] = owner * CAP + position
    total = jnp.zeros((PEERS, LANES), F32)
    lane = iota((LANES, CELLS), 0)
    rows = (anchor_ref[...].astype(F32), offsets_ref[0:1, :], offsets_ref[1:2, :])
    for part, row in enumerate(rows):
        place = (lane == part * CAP + position).astype(F32)
        total = total + dot_nt(onehot * row, place, HI)
    req_ref[...] = total


def source_kernel(x_ref, drag_ref, loss_ref, diff_ref, y_ref, z_ref, rate_s, k_s, b0_s, b1_s, x_s):
    rate_s[...] = jnp.zeros_like(rate_s)
    k_s[...] = jnp.zeros_like(k_s)
    rate_s[0:1, 0:LEV] = drag_ref[...]
    rate_s[1:5, 0:LEV] = loss_ref[...]
    k_s[0:FIELDS, 0 : LEV - 1] = diff_ref[...]
    rates = jnp.transpose(rate_s[...])
    diff = k_s[...]
    lane = iota((8, LEV_PAD), 1)
    lane_half = iota((8, LANES), 1)
    top = jnp.ones((8, LANES), F32)
    low = jnp.ones((8, LANES), F32)
    tops = [jnp.ones((8, LANES), F32)] * 2
    lows = [jnp.ones((8, LANES), F32)] * 2
    for level in range(LEV):
        if level % 12 == 11:
            low = low / top
            top = jnp.ones((8, LANES), F32)
        k = jnp.broadcast_to(diff[:, level : level + 1], (8, LANES))
        both = top + k * low
        half_at = level // LANES
        here = lane_half == level % LANES
        lows[half_at] = jnp.where(here, low, lows[half_at])
        tops[half_at] = jnp.where(here, both, tops[half_at])
        top, low = both + k * top, both
    inv = jnp.concatenate(lows, axis=1) / jnp.concatenate(tops, axis=1)
    ratio = diff * inv
    for side in (b0_s, b1_s):
        side[LEV * 8 :, :] = jnp.zeros((LEV_PAD * 8 - LEV * 8, LANES), F32)
    line = jnp.zeros((8, LEV_PAD), F32)
    for level in range(LEV - 1, -1, -1):
        factor = jnp.broadcast_to(ratio[:, level : level + 1], (8, LEV_PAD))
        line = factor * line + (lane == level).astype(F32)
        b0_s[level * 8 : level * 8 + 8, :] = line[:, :LANES]
        b1_s[level * 8 : level * 8 + 8, :] = line[:, LANES:]
    x_s[:, LEV - 1 :, :] = jnp.zeros((FIELDS, LEV_PAD - LEV + 1, 2 * CELLS), F32)
    for row in range(ROWS):
        cells = slice(row * LON, row * LON + LON)
        halves = slice(CELLS + row * LON, CELLS + row * LON + LON)

        def load(field):
            return x_ref[pl.ds(field * LEV * ROWS + row, LEV, stride=ROWS), :]

        u, v = load(0), load(1)
        speed = jnp.sqrt(u * u + v * v + 1.0)
        drag = -0.5 * rates[0:LEV, 0:1] * speed
        for field in range(FIELDS):
            if field < 2:
                value = (u, v)[field]
                half = drag * value
            else:
                value = load(field)
                half = -0.5 * rates[0:LEV, field - 1 : field] * value
            x_s[field, 0:LEV, cells] = value + half
            x_s[field, 0:LEV, halves] = half
    y_ref[FLAT - 6 :, :] = jnp.zeros((PADDED - FLAT + 6, CELLS), F32)
    z_ref[FLAT - 6 :, :] = jnp.zeros((PADDED - FLAT + 6, CELLS), F32)
    for field in range(FIELDS):
        upper = jnp.concatenate(
            [side[pl.ds(field, LEV_PAD, stride=8), :] for side in (b0_s, b1_s)], axis=1
        )
        inverse = dot_nt(upper * inv[field : field + 1, :], upper, HI)
        result = dot_nn(inverse, x_s[field], HI)
        y_ref[field * LEV : field * LEV + LEV, :] = result[0:LEV, 0:CELLS]
        z_ref[field * LEV : field * LEV + LEV, :] = result[0:LEV, CELLS:]


def owner_kernel(got_ref, y_ref, out_ref):
    got = got_ref[...]
    group = iota((PEERS, LANES), 1) // CAP
    mine = iota((PEERS, LANES), 0) % GROUPS == group
    turned = [got] + [pltpu.roll(got, n * CAP, 1) for n in range(1, GROUPS)]
    params = []
    for part in range(3):
        out = turned[(0 - part) % GROUPS]
        for n in range(1, GROUPS):
            out = jnp.where(group == n, turned[(n - part) % GROUPS], out)
        params.append(jnp.where(mine, out, 0.0))
    y_high, y_low = split_2(y_ref[...])
    place = iota((LON, LANES), 0)

    def weights(tile):
        start, lon, lat = (
            jnp.sum(part[tile * GROUPS : (tile + 1) * GROUPS, :], axis=0, keepdims=True)
            for part in params
        )
        offset = place - start.astype(jnp.int32)
        lon_weights = cubic_weights(lon)
        lat_weights = cubic_weights(lat)
        cubic = jnp.zeros((LON, LANES), F32)
        for n in range(4):
            cubic = jnp.where(offset == n, lon_weights[n], cubic)
        linear = jnp.where(offset == 1, 1.0 - lon, jnp.where(offset == 2, lon, 0.0))
        return jnp.concatenate(
            [
                lat_weights[0] * linear,
                lat_weights[1] * cubic,
                lat_weights[2] * cubic,
                lat_weights[3] * linear,
            ],
            axis=0,
        )

    for pair in range(PEERS // GROUPS // 2):
        matrix = jnp.concatenate([weights(2 * pair), weights(2 * pair + 1)], axis=1)
        m_high, m_low = split_2(matrix)
        values = dot_nn(y_high, m_high) + dot_nn(y_high, m_low) + dot_nn(y_low, m_high)
        for side in range(2):
            lanes = slice(side * LANES, side * LANES + LANES)
            parts = [values[g * CHUNK : (g + 1) * CHUNK, lanes] for g in range(GROUPS)]
            for n, block in enumerate(group_transpose(parts)):
                out_ref[(2 * pair + side) * GROUPS + n] = block


def arrive_kernel(got_ref, slot_ref, z_ref, solved_ref, top_ref, bottom_ref, west_ref, east_ref, r_s):
    for tile in range(PEERS // GROUPS):
        lanes = slice(tile * LANES, tile * LANES + LANES)
        parts = [got_ref[tile * GROUPS + n] for n in range(GROUPS)]
        for g, block in enumerate(group_transpose(parts)):
            rows = slice(g * CHUNK, (g + 1) * CHUNK)
            for piece in range(3):
                short = block.astype(BF16)
                r_s[piece, rows, lanes] = short
                block = block - short.astype(F32)
    slots = PEERS * CAP
    pick = (iota((slots, CELLS), 0) == slot_ref[...]).astype(BF16)
    solved = z_ref[...]
    solved = solved + (dot_nn(r_s[2], pick) + dot_nn(r_s[1], pick) + dot_nn(r_s[0], pick))
    solved_ref[...] = solved
    top_ref[...] = solved[:, 0:LON]
    bottom_ref[...] = solved[:, CELLS - LON :]
    row = iota((8, CELLS), 0)
    spot = iota((8, CELLS), 1)
    edge = (spot == (row % ROWS) * LON + (row // ROWS) * (LON - 1)).astype(F32)
    edges = dot_nt(edge, solved, HI)
    west_ref[...] = edges[0:ROWS]
    east_ref[...] = edges[ROWS:]


def stencil_kernel(solved_ref, north_ref, south_ref, west_ref, east_ref, stencil_ref, out_ref):
    sides = jnp.transpose(jnp.concatenate([west_ref[...], east_ref[...]], axis=0))
    lane = iota((PADDED, LON), 1)
    rows = [solved_ref[:, r * LON : (r + 1) * LON] for r in range(ROWS)]
    for r in range(ROWS):
        here = rows[r]
        north = north_ref[...] if r == 0 else rows[r - 1]
        south = south_ref[...] if r == ROWS - 1 else rows[r + 1]
        west = jnp.where(lane == 0, sides[:, r : r + 1], pltpu.roll(here, 1, 1))
        east = jnp.where(
            lane == LON - 1, sides[:, ROWS + r : ROWS + r + 1], pltpu.roll(here, LON - 1, 1)
        )
        result = here
        for n, side in enumerate((north, south, west, east)):
            result = result + stencil_ref[n * ROWS + r : n * ROWS + r + 1, :] * (side - here)
        out_ref[pl.ds(r, FLAT, stride=ROWS), :] = result[0:FLAT]


def shape_of(*dims, dtype=F32):
    return jax.ShapeDtypeStruct(dims, dtype)


def shift(cells, axis, step):
    count = lax.axis_size(axis)
    pairs = [(i, i + step) for i in range(count) if 0 <= i + step < count]
    return lax.ppermute(cells, axis, pairs)


def on_device(
    fields_in, drag_rate, loss_rate, diffusivity, owner_col, anchor_cell, offsets, stencil
):
    flat_in = fields_in.reshape(FLAT * ROWS, LON)
    request, slot_index = pl.pallas_call(
        request_kernel,
        out_shape=(shape_of(PEERS, LANES), shape_of(1, CELLS, dtype=jnp.int32)),
        name="request",
    )(owner_col.reshape(1, CELLS), anchor_cell.reshape(1, CELLS), offsets.reshape(2, CELLS))
    got = lax.all_to_all(request, "col", split_axis=0, concat_axis=0, tiled=True)
    source, local = pl.pallas_call(
        source_kernel,
        out_shape=(shape_of(PADDED, CELLS), shape_of(PADDED, CELLS)),
        scratch_shapes=[
            pltpu.VMEM((8, LEV_PAD), F32),
            pltpu.VMEM((8, LEV_PAD), F32),
            pltpu.VMEM((LEV_PAD * 8, LANES), F32),
            pltpu.VMEM((LEV_PAD * 8, LANES), F32),
            pltpu.VMEM((FIELDS, LEV_PAD, 2 * CELLS), F32),
        ],
        name="source",
    )(flat_in, drag_rate.reshape(1, LEV), loss_rate, diffusivity)
    values = pl.pallas_call(
        owner_kernel, out_shape=shape_of(PEERS, CHUNK, LANES), name="owner"
    )(got, source)
    returned = lax.all_to_all(values, "col", split_axis=0, concat_axis=0, tiled=True)
    solved, top, bottom, west, east = pl.pallas_call(
        arrive_kernel,
        out_shape=(
            shape_of(PADDED, CELLS),
            shape_of(PADDED, LON),
            shape_of(PADDED, LON),
            shape_of(ROWS, PADDED),
            shape_of(ROWS, PADDED),
        ),
        scratch_shapes=[pltpu.VMEM((3, PADDED, PEERS * CAP), BF16)],
        name="arrive",
    )(returned, slot_index, local)
    from_north = shift(bottom, "band", 1)
    from_south = shift(top, "band", -1)
    from_west = shift(east, "col", 1)
    from_east = shift(west, "col", -1)
    out = pl.pallas_call(
        stencil_kernel, out_shape=shape_of(FLAT * ROWS, LON), name="stencil"
    )(solved, from_north, from_south, from_west, from_east, stencil.reshape(4 * ROWS, LON))
    return out.reshape(fields_in.shape)


def solution(mesh):
    in_specs = (
        P(None, None, "band", "col"),
        P(),
        P(),
        P(),
        P("band", "col", None),
        P("band", "col"),
        P(None, "band", "col"),
        P(None, "band", "col"),
    )
    out_specs = P(None, None, "band", "col")
    return jax.shard_map(
        on_device, mesh=mesh, in_specs=in_specs, out_specs=out_specs, check_vma=False
    )
```

```python
from functools import partial

import jax
import jax.numpy as jnp
from jax import lax
from jax.experimental import pallas as pl
from jax.experimental.pallas import tpu as pltpu
from jax.sharding import PartitionSpec as P

F32 = jnp.float32
BF16 = jnp.bfloat16
HI = lax.Precision.HIGHEST
FIELDS = 6
LEV = 137
ROWS = 4
LON = 128
CELLS = 512
PEERS = 32
CAP = 32
LANES = 128
GROUPS = LANES // CAP
FLAT = FIELDS * LEV
CHUNK = 208
PADDED = GROUPS * CHUNK
SHARES = (208,)
STARTS = tuple(GROUPS * sum(SHARES[:n]) for n in range(len(SHARES)))
COUNTS = tuple(GROUPS * share for share in SHARES)
LEV_PAD = 256
LEV_ROWS = 144


def iota(shape, dim):
    return lax.broadcasted_iota(jnp.int32, shape, dim)


def dot_nn(a, b, precision=None):
    return lax.dot_general(
        a, b, (((1,), (0,)), ((), ())), precision=precision, preferred_element_type=F32
    )


def dot_nt(a, b, precision=None):
    return lax.dot_general(
        a, b, (((1,), (1,)), ((), ())), precision=precision, preferred_element_type=F32
    )


def cubic_weights(frac):
    return (
        -frac * (frac - 1.0) * (frac - 2.0) / 6.0,
        (frac + 1.0) * (frac - 1.0) * (frac - 2.0) / 2.0,
        -(frac + 1.0) * frac * (frac - 2.0) / 2.0,
        (frac + 1.0) * frac * (frac - 1.0) / 6.0,
    )


def split_2(x):
    high = x.astype(BF16)
    return high, (x - high.astype(F32)).astype(BF16)


def dot_split(a, b):
    a_high, a_low = split_2(a)
    b_high, b_low = split_2(b)
    return dot_nn(a_high, b_high) + dot_nn(a_high, b_low) + dot_nn(a_low, b_high)


def store_shares(refs, start, value):
    for ref, low, count in zip(refs, STARTS, COUNTS):
        first, last = max(low, start), min(low + count, start + value.shape[0])
        if first < last:
            ref[first - low : last - low, :] = value[first - start : last - start]


def half_steps(x_ref, rates, row):
    def load(field):
        return x_ref[pl.ds(field * LEV * ROWS + row, LEV, stride=ROWS), :]

    u, v = load(0), load(1)
    drag = -0.5 * rates[0:LEV, 0:1] * jnp.sqrt(u * u + v * v + 1.0)
    for field in range(FIELDS):
        value = (u, v)[field] if field < 2 else load(field)
        rate = drag if field < 2 else -0.5 * rates[0:LEV, field - 1 : field]
        yield field, value, rate * value


def solve_kernel(x_ref, rate_ref, inverse_ref, *refs, moved):
    out_refs, x_s = refs[:-1], refs[-1]
    rates = rate_ref[...]
    x_s[:, LEV - 1 :, :] = jnp.zeros((FIELDS, LEV_PAD - LEV + 1, CELLS), F32)
    for row in range(ROWS):
        for field, value, half in half_steps(x_ref, rates, row):
            x_s[field, 0:LEV, row * LON : row * LON + LON] = value + half if moved else half
    store_shares(out_refs, FLAT, jnp.zeros((PADDED - FLAT, CELLS), F32))
    for field in range(FIELDS):
        result = dot_split(inverse_ref[field], x_s[field])
        store_shares(out_refs, field * LEV, result[0:LEV])


def group_transpose(parts):
    group = iota(parts[0].shape, 1) // CAP

    def pick(choices):
        out = choices[0]
        for n in range(1, GROUPS):
            out = jnp.where(group == n, choices[n], out)
        return out

    turned = []
    for shift in range(GROUPS):
        mixed = pick([parts[(n + shift) % GROUPS] for n in range(GROUPS)])
        turned.append(pltpu.roll(mixed, shift * CAP, 1) if shift else mixed)
    return [pick([turned[(n - b) % GROUPS] for n in range(GROUPS)]) for b in range(GROUPS)]


def request_kernel(owner_ref, anchor_ref, offsets_ref, req_ref, slot_ref):
    owner = owner_ref[...]
    onehot = (iota((PEERS, CELLS), 0) == owner).astype(F32)
    earlier = (iota((CELLS, CELLS), 0) < iota((CELLS, CELLS), 1)).astype(BF16)
    before = dot_nn(onehot.astype(BF16), earlier)
    position = jnp.sum(onehot * before, axis=0, keepdims=True).astype(jnp.int32)
    slot_ref[...] = owner * CAP + position
    total = jnp.zeros((PEERS, LANES), F32)
    lane = iota((LANES, CELLS), 0)
    rows = (anchor_ref[...].astype(F32), offsets_ref[0], offsets_ref[1])
    for part, row in enumerate(rows):
        place = (lane == part * CAP + position).astype(F32)
        total = total + dot_nt(onehot * row, place, HI)
    req_ref[...] = total


def inverse_kernel(drag_ref, loss_ref, diff_ref, rate_ref, inverse_ref, rate_s, k_s, b0_s, b1_s):
    rate_s[...] = jnp.zeros_like(rate_s)
    k_s[...] = jnp.zeros_like(k_s)
    rate_s[0:1, 0:LEV] = drag_ref[...]
    rate_s[1:5, 0:LEV] = loss_ref[...]
    k_s[0:FIELDS, 0 : LEV - 1] = diff_ref[...]
    rate_ref[...] = jnp.transpose(rate_s[...])
    diff = k_s[...]
    lane = iota((8, LEV_PAD), 1)
    lane_half = iota((8, LANES), 1)
    top = jnp.ones((8, LANES), F32)
    low = jnp.ones((8, LANES), F32)
    tops = [jnp.ones((8, LANES), F32)] * 2
    lows = [jnp.ones((8, LANES), F32)] * 2
    for level in range(LEV):
        if level % 12 == 11:
            low = low / top
            top = jnp.ones((8, LANES), F32)
        k = jnp.broadcast_to(diff[:, level : level + 1], (8, LANES))
        both = top + k * low
        half_at = level // LANES
        here = lane_half == level % LANES
        lows[half_at] = jnp.where(here, low, lows[half_at])
        tops[half_at] = jnp.where(here, both, tops[half_at])
        top, low = both + k * top, both
    inv = jnp.concatenate(lows, axis=1) / jnp.concatenate(tops, axis=1)
    ratio = diff * inv
    for side in (b0_s, b1_s):
        side[LEV * 8 :, :] = jnp.zeros((LEV_PAD * 8 - LEV * 8, LANES), F32)
    line = jnp.zeros((8, LEV_PAD), F32)
    for level in range(LEV - 1, -1, -1):
        factor = jnp.broadcast_to(ratio[:, level : level + 1], (8, LEV_PAD))
        line = factor * line + (lane == level).astype(F32)
        b0_s[level * 8 : level * 8 + 8, :] = line[:, :LANES]
        b1_s[level * 8 : level * 8 + 8, :] = line[:, LANES:]
    for field in range(FIELDS):
        upper = jnp.concatenate(
            [side[pl.ds(field, LEV_PAD, stride=8), :] for side in (b0_s, b1_s)], axis=1
        )
        inverse_ref[field] = dot_nt(upper * inv[field : field + 1, :], upper, HI)[0:LEV_ROWS]


def owner_kernel(got_ref, y_ref, out_ref, high_s, low_s):
    share = out_ref.shape[1]

    @pl.when(pl.program_id(0) == 0)
    def _():
        high_s[...], low_s[...] = split_2(y_ref[...])

    got = got_ref[...]
    group = iota(got.shape, 1) // CAP
    mine = iota(got.shape, 0) % GROUPS == group
    turned = [got] + [pltpu.roll(got, n * CAP, 1) for n in range(1, GROUPS)]
    params = []
    for part in range(3):
        out = turned[(0 - part) % GROUPS]
        for n in range(1, GROUPS):
            out = jnp.where(group == n, turned[(n - part) % GROUPS], out)
        params.append(jnp.where(mine, out, 0.0))
    place = iota((LON, LANES), 0)

    def weights(tile):
        start, lon, lat = (
            jnp.sum(part[tile * GROUPS : (tile + 1) * GROUPS, :], axis=0, keepdims=True)
            for part in params
        )
        offset = place - start.astype(jnp.int32)
        lon_weights = cubic_weights(lon)
        lat_weights = cubic_weights(lat)
        cubic = jnp.zeros((LON, LANES), F32)
        for n in range(4):
            cubic = jnp.where(offset == n, lon_weights[n], cubic)
        linear = jnp.where(offset == 1, 1.0 - lon, jnp.where(offset == 2, lon, 0.0))
        return jnp.concatenate(
            [
                lat_weights[0] * linear,
                lat_weights[1] * cubic,
                lat_weights[2] * cubic,
                lat_weights[3] * linear,
            ],
            axis=0,
        )

    matrix = jnp.concatenate([weights(0), weights(1)], axis=1)
    m_high, m_low = split_2(matrix)
    values = dot_nn(high_s[...], m_high) + dot_nn(high_s[...], m_low) + dot_nn(low_s[...], m_high)
    for side in range(2):
        lanes = slice(side * LANES, side * LANES + LANES)
        parts = [values[g * share : (g + 1) * share, lanes] for g in range(GROUPS)]
        for n, block in enumerate(group_transpose(parts)):
            out_ref[side * GROUPS + n] = block


def arrive_kernel(got_ref, slot_ref, z_ref, solved_ref, top_ref, bottom_ref, west_ref, east_ref, r_s, g_s, sems):
    share = got_ref.shape[1]
    copies = [
        pltpu.make_async_copy(
            got_ref.at[pl.ds(tile * GROUPS, GROUPS)],
            g_s.at[pl.ds(tile * GROUPS, GROUPS)],
            sems.at[tile],
        )
        for tile in range(PEERS // GROUPS)
    ]
    for copy in copies:
        copy.start()
    for tile in range(PEERS // GROUPS):
        lanes = slice(tile * LANES, tile * LANES + LANES)
        copies[tile].wait()
        parts = [g_s[tile * GROUPS + n] for n in range(GROUPS)]
        for g, block in enumerate(group_transpose(parts)):
            rows = slice(g * share, (g + 1) * share)
            for piece in range(2):
                short = block.astype(BF16)
                r_s[piece, rows, lanes] = short
                block = block - short.astype(F32)
    slots = PEERS * CAP
    pick = (iota((slots, CELLS), 0) == slot_ref[...]).astype(BF16)
    solved = z_ref[...]
    solved = solved + (dot_nn(r_s[1], pick) + dot_nn(r_s[0], pick))
    solved_ref[...] = solved
    top_ref[...] = solved[:, 0:LON]
    bottom_ref[...] = solved[:, CELLS - LON :]
    row = iota((8, CELLS), 0)
    spot = iota((8, CELLS), 1)
    edge = (spot == (row % ROWS) * LON + (row // ROWS) * (LON - 1)).astype(F32)
    edges = dot_nt(edge, solved, HI)
    west_ref[...] = edges[0:ROWS]
    east_ref[...] = edges[ROWS:]


def stencil_kernel(
    solved_ref, north_ref, south_ref, west_ref, east_ref, stencil_ref, *rest, start, count
):
    out_ref, block_s, sems = rest[-3:]
    sides = jnp.transpose(jnp.concatenate([west_ref[...], east_ref[...]], axis=0))
    copies = []
    for part, low in enumerate(range(0, count, CHUNK)):
        size = min(CHUNK, count - low)
        used = slice(low, low + size)
        lane = iota((size, LON), 1)
        rows = [solved_ref[used, r * LON : (r + 1) * LON] for r in range(ROWS)]
        for r in range(ROWS):
            here = rows[r]
            north = north_ref[used, :] if r == 0 else rows[r - 1]
            south = south_ref[used, :] if r == ROWS - 1 else rows[r + 1]
            west = jnp.where(lane == 0, sides[used, r : r + 1], pltpu.roll(here, 1, 1))
            east = jnp.where(
                lane == LON - 1,
                sides[used, ROWS + r : ROWS + r + 1],
                pltpu.roll(here, LON - 1, 1),
            )
            result = here
            for n, side in enumerate((north, south, west, east)):
                coef = stencil_ref[n * ROWS + r : n * ROWS + r + 1, :]
                result = result + coef * (side - here)
            block_s[pl.ds(low * ROWS + r, size, stride=ROWS), :] = result
        copy = pltpu.make_async_copy(
            block_s.at[pl.ds(low * ROWS, size * ROWS), :],
            out_ref.at[pl.ds((start + low) * ROWS, size * ROWS), :],
            sems.at[part],
        )
        copy.start()
        copies.append(copy)
    for copy in copies:
        copy.wait()


def shape_of(*dims, dtype=F32):
    return jax.ShapeDtypeStruct(dims, dtype)


def shift(cells, axis, step):
    count = lax.axis_size(axis)
    pairs = [(i, i + step) for i in range(count) if 0 <= i + step < count]
    return lax.ppermute(cells, axis, pairs)


def on_device(
    fields_in, drag_rate, loss_rate, diffusivity, owner_col, anchor_cell, offsets, stencil
):
    flat_in = fields_in.reshape(FLAT * ROWS, LON)
    request, slot_index = pl.pallas_call(
        request_kernel,
        out_shape=(shape_of(PEERS, LANES), shape_of(1, CELLS, dtype=jnp.int32)),
        name="request",
    )(owner_col.reshape(1, CELLS), anchor_cell.reshape(1, CELLS), offsets)
    got = lax.all_to_all(request, "col", split_axis=0, concat_axis=0, tiled=True)
    rates, inverse = pl.pallas_call(
        inverse_kernel,
        out_shape=(shape_of(LEV_PAD, 8), shape_of(FIELDS, LEV_ROWS, LEV_PAD)),
        scratch_shapes=[
            pltpu.VMEM((8, LEV_PAD), F32),
            pltpu.VMEM((8, LEV_PAD), F32),
            pltpu.VMEM((LEV_PAD * 8, LANES), F32),
            pltpu.VMEM((LEV_PAD * 8, LANES), F32),
        ],
        name="inverse",
    )(drag_rate.reshape(1, LEV), loss_rate, diffusivity)

    def solve(moved):
        return pl.pallas_call(
            partial(solve_kernel, moved=moved),
            out_shape=tuple(shape_of(count, CELLS) for count in COUNTS),
            scratch_shapes=[pltpu.VMEM((FIELDS, LEV_PAD, CELLS), F32)],
            name="solve_moved" if moved else "solve_half",
        )(flat_in, rates, inverse)

    sources = solve(True)
    returned = []
    for share, source in zip(SHARES, sources):
        values = pl.pallas_call(
            owner_kernel,
            grid=(PEERS // GROUPS // 2,),
            in_specs=[
                pl.BlockSpec((2 * GROUPS, LANES), lambda i: (i, 0)),
                pl.BlockSpec((GROUPS * share, CELLS), lambda i: (0, 0)),
            ],
            out_specs=pl.BlockSpec((2 * GROUPS, share, LANES), lambda i: (i, 0, 0)),
            out_shape=shape_of(PEERS, share, LANES),
            scratch_shapes=[pltpu.VMEM((GROUPS * share, CELLS), BF16)] * 2,
            name="owner",
        )(got, source)
        returned.append(
            lax.all_to_all(values, "col", split_axis=0, concat_axis=0, tiled=True)
        )
    locals_ = solve(False)
    coefs = stencil.reshape(4 * ROWS, LON)
    out = None
    for start, count, back, local in zip(STARTS, COUNTS, returned, locals_):
        solved, top, bottom, west, east = pl.pallas_call(
            arrive_kernel,
            in_specs=[pl.BlockSpec(memory_space=pl.ANY)]
            + [pl.BlockSpec(memory_space=pltpu.VMEM)] * 2,
            out_shape=(
                shape_of(count, CELLS),
                shape_of(count, LON),
                shape_of(count, LON),
                shape_of(ROWS, count),
                shape_of(ROWS, count),
            ),
            scratch_shapes=[
                pltpu.VMEM((2, count, PEERS * CAP), BF16),
                pltpu.VMEM((PEERS, share, LANES), F32),
                pltpu.SemaphoreType.DMA((PEERS // GROUPS,)),
            ],
            name="arrive",
        )(back, slot_index, local)
        from_north = shift(bottom, "band", 1)
        from_south = shift(top, "band", -1)
        from_west = shift(east, "col", 1)
        from_east = shift(west, "col", -1)
        used = min(count, FLAT - start)
        whole = [] if out is None else [out]
        out = pl.pallas_call(
            partial(stencil_kernel, start=start, count=used),
            out_shape=shape_of(FLAT * ROWS, LON),
            in_specs=[pl.BlockSpec(memory_space=pltpu.VMEM)] * 6
            + [pl.BlockSpec(memory_space=pl.ANY)] * len(whole),
            out_specs=pl.BlockSpec(memory_space=pl.ANY),
            scratch_shapes=[pltpu.VMEM((used * ROWS, LON), F32), pltpu.SemaphoreType.DMA((GROUPS,))],
            input_output_aliases={6: 0} if whole else {},
            name="stencil",
        )(solved, from_north, from_south, from_west, from_east, coefs, *whole)
    return out.reshape(fields_in.shape)


def solution(mesh):
    in_specs = (
        P(None, None, "band", "col"),
        P(),
        P(),
        P(),
        P("band", "col", None),
        P("band", "col"),
        P(None, "band", "col"),
        P(None, "band", "col"),
    )
    out_specs = P(None, None, "band", "col")
    return jax.shard_map(
        on_device, mesh=mesh, in_specs=in_specs, out_specs=out_specs, check_vma=False
    )
```

```python
from functools import partial

import jax
import jax.numpy as jnp
from jax import lax
from jax.experimental import pallas as pl
from jax.experimental.pallas import tpu as pltpu
from jax.sharding import PartitionSpec as P

F32 = jnp.float32
BF16 = jnp.bfloat16
HI = lax.Precision.HIGHEST
FIELDS = 6
LEV = 137
ROWS = 4
LON = 128
CELLS = 512
PEERS = 32
CAP = 32
LANES = 128
GROUPS = LANES // CAP
FLAT = FIELDS * LEV
CHUNK = 208
PADDED = GROUPS * CHUNK
SHARES = (208,)
STARTS = tuple(GROUPS * sum(SHARES[:n]) for n in range(len(SHARES)))
COUNTS = tuple(GROUPS * share for share in SHARES)
LEV_PAD = 256
LEV_ROWS = 144


def iota(shape, dim):
    return lax.broadcasted_iota(jnp.int32, shape, dim)


def dot_nn(a, b, precision=None):
    return lax.dot_general(
        a, b, (((1,), (0,)), ((), ())), precision=precision, preferred_element_type=F32
    )


def dot_nt(a, b, precision=None):
    return lax.dot_general(
        a, b, (((1,), (1,)), ((), ())), precision=precision, preferred_element_type=F32
    )


def cubic_weights(frac):
    return (
        -frac * (frac - 1.0) * (frac - 2.0) / 6.0,
        (frac + 1.0) * (frac - 1.0) * (frac - 2.0) / 2.0,
        -(frac + 1.0) * frac * (frac - 2.0) / 2.0,
        (frac + 1.0) * frac * (frac - 1.0) / 6.0,
    )


def split_2(x):
    high = x.astype(BF16)
    return high, (x - high.astype(F32)).astype(BF16)


def dot_split(a, b):
    a_high, a_low = split_2(a)
    b_high, b_low = split_2(b)
    return dot_nn(a_high, b_high) + dot_nn(a_high, b_low) + dot_nn(a_low, b_high)


def store_shares(refs, start, value):
    for ref, low, count in zip(refs, STARTS, COUNTS):
        first, last = max(low, start), min(low + count, start + value.shape[0])
        if first < last:
            ref[first - low : last - low, :] = value[first - start : last - start]


def half_steps(x_ref, rates, row):
    def load(field):
        return x_ref[pl.ds(field * LEV * ROWS + row, LEV, stride=ROWS), :]

    u, v = load(0), load(1)
    drag = -0.5 * rates[0:LEV, 0:1] * jnp.sqrt(u * u + v * v + 1.0)
    for field in range(FIELDS):
        value = (u, v)[field] if field < 2 else load(field)
        rate = drag if field < 2 else -0.5 * rates[0:LEV, field - 1 : field]
        yield field, value, rate * value


def solve_kernel(x_ref, rate_ref, inverse_ref, *refs, moved):
    out_refs, x_s = refs[:-1], refs[-1]
    rates = rate_ref[...]
    x_s[:, LEV - 1 :, :] = jnp.zeros((FIELDS, LEV_PAD - LEV + 1, CELLS), F32)
    for row in range(ROWS):
        for field, value, half in half_steps(x_ref, rates, row):
            x_s[field, 0:LEV, row * LON : row * LON + LON] = value + half if moved else half
    store_shares(out_refs, FLAT, jnp.zeros((PADDED - FLAT, CELLS), F32))
    for field in range(FIELDS):
        result = dot_split(inverse_ref[field], x_s[field])
        store_shares(out_refs, field * LEV, result[0:LEV])


def group_transpose(parts):
    group = iota(parts[0].shape, 1) // CAP

    def pick(choices):
        out = choices[0]
        for n in range(1, GROUPS):
            out = jnp.where(group == n, choices[n], out)
        return out

    turned = []
    for shift in range(GROUPS):
        mixed = pick([parts[(n + shift) % GROUPS] for n in range(GROUPS)])
        turned.append(pltpu.roll(mixed, shift * CAP, 1) if shift else mixed)
    return [pick([turned[(n - b) % GROUPS] for n in range(GROUPS)]) for b in range(GROUPS)]


def request_kernel(owner_ref, anchor_ref, offsets_ref, req_ref, slot_ref):
    owner = owner_ref[...]
    onehot = (iota((PEERS, CELLS), 0) == owner).astype(F32)
    earlier = (iota((CELLS, CELLS), 0) < iota((CELLS, CELLS), 1)).astype(BF16)
    before = dot_nn(onehot.astype(BF16), earlier)
    position = jnp.sum(onehot * before, axis=0, keepdims=True).astype(jnp.int32)
    slot_ref[...] = owner * CAP + position
    total = jnp.zeros((PEERS, LANES), F32)
    lane = iota((LANES, CELLS), 0)
    rows = (anchor_ref[...].astype(F32), offsets_ref[0], offsets_ref[1])
    for part, row in enumerate(rows):
        place = (lane == part * CAP + position).astype(F32)
        total = total + dot_nt(onehot * row, place, HI)
    req_ref[...] = total


def inverse_kernel(drag_ref, loss_ref, diff_ref, rate_ref, inverse_ref, rate_s, k_s, b0_s, b1_s):
    rate_s[...] = jnp.zeros_like(rate_s)
    k_s[...] = jnp.zeros_like(k_s)
    rate_s[0:1, 0:LEV] = drag_ref[...]
    rate_s[1:5, 0:LEV] = loss_ref[...]
    k_s[0:FIELDS, 0 : LEV - 1] = diff_ref[...]
    rate_ref[...] = jnp.transpose(rate_s[...])
    diff = k_s[...]
    lane = iota((8, LEV_PAD), 1)
    lane_half = iota((8, LANES), 1)
    top = jnp.ones((8, LANES), F32)
    low = jnp.ones((8, LANES), F32)
    tops = [jnp.ones((8, LANES), F32)] * 2
    lows = [jnp.ones((8, LANES), F32)] * 2
    for level in range(LEV):
        if level % 12 == 11:
            low = low / top
            top = jnp.ones((8, LANES), F32)
        k = jnp.broadcast_to(diff[:, level : level + 1], (8, LANES))
        both = top + k * low
        half_at = level // LANES
        here = lane_half == level % LANES
        lows[half_at] = jnp.where(here, low, lows[half_at])
        tops[half_at] = jnp.where(here, both, tops[half_at])
        top, low = both + k * top, both
    inv = jnp.concatenate(lows, axis=1) / jnp.concatenate(tops, axis=1)
    ratio = diff * inv
    for side in (b0_s, b1_s):
        side[LEV * 8 :, :] = jnp.zeros((LEV_PAD * 8 - LEV * 8, LANES), F32)
    line = jnp.zeros((8, LEV_PAD), F32)
    for level in range(LEV - 1, -1, -1):
        factor = jnp.broadcast_to(ratio[:, level : level + 1], (8, LEV_PAD))
        line = factor * line + (lane == level).astype(F32)
        b0_s[level * 8 : level * 8 + 8, :] = line[:, :LANES]
        b1_s[level * 8 : level * 8 + 8, :] = line[:, LANES:]
    for field in range(FIELDS):
        upper = jnp.concatenate(
            [side[pl.ds(field, LEV_PAD, stride=8), :] for side in (b0_s, b1_s)], axis=1
        )
        inverse_ref[field] = dot_nt(upper * inv[field : field + 1, :], upper, HI)[0:LEV_ROWS]


def owner_kernel(got_ref, y_ref, out_ref, high_s, low_s):
    share = out_ref.shape[1]

    @pl.when(pl.program_id(0) == 0)
    def _():
        high_s[...], low_s[...] = split_2(y_ref[...])

    got = got_ref[...]
    group = iota(got.shape, 1) // CAP
    mine = iota(got.shape, 0) % GROUPS == group
    turned = [got] + [pltpu.roll(got, n * CAP, 1) for n in range(1, GROUPS)]
    params = []
    for part in range(3):
        out = turned[(0 - part) % GROUPS]
        for n in range(1, GROUPS):
            out = jnp.where(group == n, turned[(n - part) % GROUPS], out)
        params.append(jnp.where(mine, out, 0.0))
    place = iota((LON, LANES), 0)

    def weights(tile):
        start, lon, lat = (
            jnp.sum(part[tile * GROUPS : (tile + 1) * GROUPS, :], axis=0, keepdims=True)
            for part in params
        )
        offset = place - start.astype(jnp.int32)
        lon_weights = cubic_weights(lon)
        lat_weights = cubic_weights(lat)
        cubic = jnp.zeros((LON, LANES), F32)
        for n in range(4):
            cubic = jnp.where(offset == n, lon_weights[n], cubic)
        linear = jnp.where(offset == 1, 1.0 - lon, jnp.where(offset == 2, lon, 0.0))
        return jnp.concatenate(
            [
                lat_weights[0] * linear,
                lat_weights[1] * cubic,
                lat_weights[2] * cubic,
                lat_weights[3] * linear,
            ],
            axis=0,
        )

    matrix = jnp.concatenate([weights(0), weights(1)], axis=1)
    m_high, m_low = split_2(matrix)
    values = dot_nn(high_s[...], m_high) + dot_nn(high_s[...], m_low) + dot_nn(low_s[...], m_high)
    for side in range(2):
        lanes = slice(side * LANES, side * LANES + LANES)
        parts = [values[g * share : (g + 1) * share, lanes] for g in range(GROUPS)]
        for n, block in enumerate(group_transpose(parts)):
            out_ref[side * GROUPS + n] = block


def arrive_kernel(got_ref, slot_ref, z_ref, solved_ref, top_ref, bottom_ref, west_ref, east_ref, r_s, g_s, sems):
    share = got_ref.shape[1]
    copies = [
        pltpu.make_async_copy(
            got_ref.at[pl.ds(tile * GROUPS, GROUPS)],
            g_s.at[pl.ds(tile * GROUPS, GROUPS)],
            sems.at[tile],
        )
        for tile in range(PEERS // GROUPS)
    ]
    for copy in copies:
        copy.start()
    for tile in range(PEERS // GROUPS):
        lanes = slice(tile * LANES, tile * LANES + LANES)
        copies[tile].wait()
        parts = [g_s[tile * GROUPS + n] for n in range(GROUPS)]
        for g, block in enumerate(group_transpose(parts)):
            rows = slice(g * share, (g + 1) * share)
            for piece in range(2):
                short = block.astype(BF16)
                r_s[piece, rows, lanes] = short
                block = block - short.astype(F32)
    slots = PEERS * CAP
    pick = (iota((slots, CELLS), 0) == slot_ref[...]).astype(BF16)
    solved = z_ref[...]
    solved = solved + (dot_nn(r_s[1], pick) + dot_nn(r_s[0], pick))
    solved_ref[...] = solved
    top_ref[...] = solved[:, 0:LON]
    bottom_ref[...] = solved[:, CELLS - LON :]
    row = iota((8, CELLS), 0)
    spot = iota((8, CELLS), 1)
    edge = (spot == (row % ROWS) * LON + (row // ROWS) * (LON - 1)).astype(F32)
    edges = dot_nt(edge, solved, HI)
    west_ref[...] = edges[0:ROWS]
    east_ref[...] = edges[ROWS:]


def stencil_kernel(
    solved_ref, north_ref, south_ref, west_ref, east_ref, stencil_ref, *rest, start, count
):
    out_ref, block_s, sems = rest[-3:]
    sides = jnp.transpose(jnp.concatenate([west_ref[...], east_ref[...]], axis=0))
    copies = []
    for part, low in enumerate(range(0, count, CHUNK)):
        size = min(CHUNK, count - low)
        used = slice(low, low + size)
        lane = iota((size, LON), 1)
        rows = [solved_ref[used, r * LON : (r + 1) * LON] for r in range(ROWS)]
        for r in range(ROWS):
            here = rows[r]
            north = north_ref[used, :] if r == 0 else rows[r - 1]
            south = south_ref[used, :] if r == ROWS - 1 else rows[r + 1]
            west = jnp.where(lane == 0, sides[used, r : r + 1], pltpu.roll(here, 1, 1))
            east = jnp.where(
                lane == LON - 1,
                sides[used, ROWS + r : ROWS + r + 1],
                pltpu.roll(here, LON - 1, 1),
            )
            result = here
            for n, side in enumerate((north, south, west, east)):
                coef = stencil_ref[n * ROWS + r : n * ROWS + r + 1, :]
                result = result + coef * (side - here)
            block_s[pl.ds(low * ROWS + r, size, stride=ROWS), :] = result
        copy = pltpu.make_async_copy(
            block_s.at[pl.ds(low * ROWS, size * ROWS), :],
            out_ref.at[pl.ds((start + low) * ROWS, size * ROWS), :],
            sems.at[part],
        )
        copy.start()
        copies.append(copy)
    for copy in copies:
        copy.wait()


def shape_of(*dims, dtype=F32):
    return jax.ShapeDtypeStruct(dims, dtype)


def shift(cells, axis, step):
    count = lax.axis_size(axis)
    pairs = [(i, i + step) for i in range(count) if 0 <= i + step < count]
    return lax.ppermute(cells, axis, pairs)


def on_device(
    fields_in, drag_rate, loss_rate, diffusivity, owner_col, anchor_cell, offsets, stencil
):
    flat_in = fields_in.reshape(FLAT * ROWS, LON)
    request, slot_index = pl.pallas_call(
        request_kernel,
        out_shape=(shape_of(PEERS, LANES), shape_of(1, CELLS, dtype=jnp.int32)),
        name="request",
    )(owner_col.reshape(1, CELLS), anchor_cell.reshape(1, CELLS), offsets)
    got = lax.all_to_all(request, "col", split_axis=0, concat_axis=0, tiled=True)
    rates, inverse = pl.pallas_call(
        inverse_kernel,
        out_shape=(shape_of(LEV_PAD, 8), shape_of(FIELDS, LEV_ROWS, LEV_PAD)),
        scratch_shapes=[
            pltpu.VMEM((8, LEV_PAD), F32),
            pltpu.VMEM((8, LEV_PAD), F32),
            pltpu.VMEM((LEV_PAD * 8, LANES), F32),
            pltpu.VMEM((LEV_PAD * 8, LANES), F32),
        ],
        name="inverse",
    )(drag_rate.reshape(1, LEV), loss_rate, diffusivity)

    def solve(moved):
        return pl.pallas_call(
            partial(solve_kernel, moved=moved),
            out_shape=tuple(shape_of(count, CELLS) for count in COUNTS),
            scratch_shapes=[pltpu.VMEM((FIELDS, LEV_PAD, CELLS), F32)],
            compiler_params=None if moved else pltpu.CompilerParams(vmem_limit_bytes=65_000_000),
            name="solve_moved" if moved else "solve_half",
        )(flat_in, rates, inverse)

    sources = solve(True)
    returned = []
    for share, source in zip(SHARES, sources):
        values = pl.pallas_call(
            owner_kernel,
            grid=(PEERS // GROUPS // 2,),
            in_specs=[
                pl.BlockSpec((2 * GROUPS, LANES), lambda i: (i, 0)),
                pl.BlockSpec((GROUPS * share, CELLS), lambda i: (0, 0)),
            ],
            out_specs=pl.BlockSpec((2 * GROUPS, share, LANES), lambda i: (i, 0, 0)),
            out_shape=shape_of(PEERS, share, LANES),
            scratch_shapes=[pltpu.VMEM((GROUPS * share, CELLS), BF16)] * 2,
            name="owner",
        )(got, source)
        returned.append(
            lax.all_to_all(values, "col", split_axis=0, concat_axis=0, tiled=True)
        )
    locals_ = solve(False)
    coefs = stencil.reshape(4 * ROWS, LON)
    out = None
    for start, count, back, local in zip(STARTS, COUNTS, returned, locals_):
        solved, top, bottom, west, east = pl.pallas_call(
            arrive_kernel,
            in_specs=[pl.BlockSpec(memory_space=pl.ANY)]
            + [pl.BlockSpec(memory_space=pltpu.VMEM)] * 2,
            out_shape=(
                shape_of(count, CELLS),
                shape_of(count, LON),
                shape_of(count, LON),
                shape_of(ROWS, count),
                shape_of(ROWS, count),
            ),
            scratch_shapes=[
                pltpu.VMEM((2, count, PEERS * CAP), BF16),
                pltpu.VMEM((PEERS, share, LANES), F32),
                pltpu.SemaphoreType.DMA((PEERS // GROUPS,)),
            ],
            name="arrive",
        )(back, slot_index, local)
        from_north = shift(bottom, "band", 1)
        from_south = shift(top, "band", -1)
        from_west = shift(east, "col", 1)
        from_east = shift(west, "col", -1)
        used = min(count, FLAT - start)
        whole = [] if out is None else [out]
        out = pl.pallas_call(
            partial(stencil_kernel, start=start, count=used),
            out_shape=shape_of(FLAT * ROWS, LON),
            in_specs=[pl.BlockSpec(memory_space=pltpu.VMEM)] * 6
            + [pl.BlockSpec(memory_space=pl.ANY)] * len(whole),
            out_specs=pl.BlockSpec(memory_space=pl.ANY),
            scratch_shapes=[pltpu.VMEM((used * ROWS, LON), F32), pltpu.SemaphoreType.DMA((GROUPS,))],
            input_output_aliases={6: 0} if whole else {},
            name="stencil",
        )(solved, from_north, from_south, from_west, from_east, coefs, *whole)
    return out.reshape(fields_in.shape)


def solution(mesh):
    in_specs = (
        P(None, None, "band", "col"),
        P(),
        P(),
        P(),
        P("band", "col", None),
        P("band", "col"),
        P(None, "band", "col"),
        P(None, "band", "col"),
    )
    out_specs = P(None, None, "band", "col")
    return jax.shard_map(
        on_device, mesh=mesh, in_specs=in_specs, out_specs=out_specs, check_vma=False
    )
```

```python
from functools import partial

import jax
import jax.numpy as jnp
from jax import lax
from jax.experimental import pallas as pl
from jax.experimental.pallas import tpu as pltpu
from jax.sharding import PartitionSpec as P

F32 = jnp.float32
BF16 = jnp.bfloat16
HI = lax.Precision.HIGHEST
FIELDS = 6
LEV = 137
ROWS = 4
LON = 128
CELLS = 512
PEERS = 32
CAP = 32
LANES = 128
GROUPS = LANES // CAP
FLAT = FIELDS * LEV
CHUNK = 208
PADDED = GROUPS * CHUNK
SHARES = (208,)
STARTS = tuple(GROUPS * sum(SHARES[:n]) for n in range(len(SHARES)))
COUNTS = tuple(GROUPS * share for share in SHARES)
LEV_PAD = 256
LEV_ROWS = 144


def iota(shape, dim):
    return lax.broadcasted_iota(jnp.int32, shape, dim)


def dot_nn(a, b, precision=None):
    return lax.dot_general(
        a, b, (((1,), (0,)), ((), ())), precision=precision, preferred_element_type=F32
    )


def dot_nt(a, b, precision=None):
    return lax.dot_general(
        a, b, (((1,), (1,)), ((), ())), precision=precision, preferred_element_type=F32
    )


def cubic_weights(frac):
    return (
        -frac * (frac - 1.0) * (frac - 2.0) / 6.0,
        (frac + 1.0) * (frac - 1.0) * (frac - 2.0) / 2.0,
        -(frac + 1.0) * frac * (frac - 2.0) / 2.0,
        (frac + 1.0) * frac * (frac - 1.0) / 6.0,
    )


def split_2(x):
    high = x.astype(BF16)
    return high, (x - high.astype(F32)).astype(BF16)


def dot_split(a, b):
    a_high, a_low = split_2(a)
    b_high, b_low = split_2(b)
    return dot_nn(a_high, b_high) + dot_nn(a_high, b_low) + dot_nn(a_low, b_high)


def store_shares(refs, start, value):
    for ref, low, count in zip(refs, STARTS, COUNTS):
        first, last = max(low, start), min(low + count, start + value.shape[0])
        if first < last:
            ref[first - low : last - low, :] = value[first - start : last - start]


def half_steps(x_ref, rates, row):
    def load(field):
        return x_ref[pl.ds(field * LEV * ROWS + row, LEV, stride=ROWS), :]

    u, v = load(0), load(1)
    drag = -0.5 * rates[0:LEV, 0:1] * jnp.sqrt(u * u + v * v + 1.0)
    for field in range(FIELDS):
        value = (u, v)[field] if field < 2 else load(field)
        rate = drag if field < 2 else -0.5 * rates[0:LEV, field - 1 : field]
        yield field, value, rate * value


def solve_kernel(x_ref, rate_ref, inverse_ref, *refs, moved):
    out_refs, x_s = refs[:-1], refs[-1]
    rates = rate_ref[...]
    x_s[:, LEV - 1 :, :] = jnp.zeros((FIELDS, LEV_PAD - LEV + 1, CELLS), F32)
    for row in range(ROWS):
        for field, value, half in half_steps(x_ref, rates, row):
            x_s[field, 0:LEV, row * LON : row * LON + LON] = value + half if moved else half
    store_shares(out_refs, FLAT, jnp.zeros((PADDED - FLAT, CELLS), F32))
    for field in range(FIELDS):
        result = dot_split(inverse_ref[field], x_s[field])
        store_shares(out_refs, field * LEV, result[0:LEV])


def group_transpose(parts):
    group = iota(parts[0].shape, 1) // CAP

    def pick(choices):
        out = choices[0]
        for n in range(1, GROUPS):
            out = jnp.where(group == n, choices[n], out)
        return out

    turned = []
    for shift in range(GROUPS):
        mixed = pick([parts[(n + shift) % GROUPS] for n in range(GROUPS)])
        turned.append(pltpu.roll(mixed, shift * CAP, 1) if shift else mixed)
    return [pick([turned[(n - b) % GROUPS] for n in range(GROUPS)]) for b in range(GROUPS)]


def request_kernel(owner_ref, anchor_ref, offsets_ref, req_ref, slot_ref):
    owner = owner_ref[...]
    onehot = (iota((PEERS, CELLS), 0) == owner).astype(F32)
    earlier = (iota((CELLS, CELLS), 0) < iota((CELLS, CELLS), 1)).astype(BF16)
    before = dot_nn(onehot.astype(BF16), earlier)
    position = jnp.sum(onehot * before, axis=0, keepdims=True).astype(jnp.int32)
    slot_ref[...] = owner * CAP + position
    total = jnp.zeros((PEERS, LANES), F32)
    lane = iota((LANES, CELLS), 0)
    rows = (anchor_ref[...].astype(F32), offsets_ref[0], offsets_ref[1])
    for part, row in enumerate(rows):
        place = (lane == part * CAP + position).astype(F32)
        total = total + dot_nt(onehot * row, place, HI)
    req_ref[...] = total


def inverse_kernel(drag_ref, loss_ref, diff_ref, rate_ref, inverse_ref, rate_s, k_s, b0_s, b1_s):
    rate_s[...] = jnp.zeros_like(rate_s)
    k_s[...] = jnp.zeros_like(k_s)
    rate_s[0:1, 0:LEV] = drag_ref[...]
    rate_s[1:5, 0:LEV] = loss_ref[...]
    k_s[0:FIELDS, 0 : LEV - 1] = diff_ref[...]
    rate_ref[...] = jnp.transpose(rate_s[...])
    diff = k_s[...]
    lane = iota((8, LEV_PAD), 1)
    lane_half = iota((8, LANES), 1)
    top = jnp.ones((8, LANES), F32)
    low = jnp.ones((8, LANES), F32)
    tops = [jnp.ones((8, LANES), F32)] * 2
    lows = [jnp.ones((8, LANES), F32)] * 2
    for level in range(LEV):
        if level % 12 == 11:
            low = low / top
            top = jnp.ones((8, LANES), F32)
        k = jnp.broadcast_to(diff[:, level : level + 1], (8, LANES))
        both = top + k * low
        half_at = level // LANES
        here = lane_half == level % LANES
        lows[half_at] = jnp.where(here, low, lows[half_at])
        tops[half_at] = jnp.where(here, both, tops[half_at])
        top, low = both + k * top, both
    inv = jnp.concatenate(lows, axis=1) / jnp.concatenate(tops, axis=1)
    ratio = diff * inv
    for side in (b0_s, b1_s):
        side[LEV * 8 :, :] = jnp.zeros((LEV_PAD * 8 - LEV * 8, LANES), F32)
    line = jnp.zeros((8, LEV_PAD), F32)
    for level in range(LEV - 1, -1, -1):
        factor = jnp.broadcast_to(ratio[:, level : level + 1], (8, LEV_PAD))
        line = factor * line + (lane == level).astype(F32)
        b0_s[level * 8 : level * 8 + 8, :] = line[:, :LANES]
        b1_s[level * 8 : level * 8 + 8, :] = line[:, LANES:]
    for field in range(FIELDS):
        upper = jnp.concatenate(
            [side[pl.ds(field, LEV_PAD, stride=8), :] for side in (b0_s, b1_s)], axis=1
        )
        inverse_ref[field] = dot_nt(upper * inv[field : field + 1, :], upper, HI)[0:LEV_ROWS]


def owner_kernel(got_ref, y_ref, out_ref, high_s, low_s):
    share = out_ref.shape[1]

    @pl.when(pl.program_id(0) == 0)
    def _():
        high_s[...], low_s[...] = split_2(y_ref[...])

    got = got_ref[...]
    group = iota(got.shape, 1) // CAP
    mine = iota(got.shape, 0) % GROUPS == group
    turned = [got] + [pltpu.roll(got, n * CAP, 1) for n in range(1, GROUPS)]
    params = []
    for part in range(3):
        out = turned[(0 - part) % GROUPS]
        for n in range(1, GROUPS):
            out = jnp.where(group == n, turned[(n - part) % GROUPS], out)
        params.append(jnp.where(mine, out, 0.0))
    place = iota((LON, LANES), 0)

    def weights(tile):
        start, lon, lat = (
            jnp.sum(part[tile * GROUPS : (tile + 1) * GROUPS, :], axis=0, keepdims=True)
            for part in params
        )
        offset = place - start.astype(jnp.int32)
        lon_weights = cubic_weights(lon)
        lat_weights = cubic_weights(lat)
        cubic = jnp.zeros((LON, LANES), F32)
        for n in range(4):
            cubic = jnp.where(offset == n, lon_weights[n], cubic)
        linear = jnp.where(offset == 1, 1.0 - lon, jnp.where(offset == 2, lon, 0.0))
        return jnp.concatenate(
            [
                lat_weights[0] * linear,
                lat_weights[1] * cubic,
                lat_weights[2] * cubic,
                lat_weights[3] * linear,
            ],
            axis=0,
        )

    matrix = jnp.concatenate([weights(0), weights(1)], axis=1)
    m_high, m_low = split_2(matrix)
    values = dot_nn(high_s[...], m_high) + dot_nn(high_s[...], m_low) + dot_nn(low_s[...], m_high)
    for side in range(2):
        lanes = slice(side * LANES, side * LANES + LANES)
        parts = [values[g * share : (g + 1) * share, lanes] for g in range(GROUPS)]
        for n, block in enumerate(group_transpose(parts)):
            out_ref[side * GROUPS + n] = block


def arrive_kernel(got_ref, slot_ref, z_ref, solved_ref, top_ref, bottom_ref, west_ref, east_ref, r_s, g_s, sems):
    share = got_ref.shape[1]
    copies = [
        pltpu.make_async_copy(
            got_ref.at[pl.ds(tile * GROUPS, GROUPS)],
            g_s.at[pl.ds(tile * GROUPS, GROUPS)],
            sems.at[tile],
        )
        for tile in range(PEERS // GROUPS)
    ]
    for copy in copies:
        copy.start()
    for tile in range(PEERS // GROUPS):
        lanes = slice(tile * LANES, tile * LANES + LANES)
        copies[tile].wait()
        parts = [g_s[tile * GROUPS + n] for n in range(GROUPS)]
        for g, block in enumerate(group_transpose(parts)):
            rows = slice(g * share, (g + 1) * share)
            for piece in range(2):
                short = block.astype(BF16)
                r_s[piece, rows, lanes] = short
                block = block - short.astype(F32)
    slots = PEERS * CAP
    pick = (iota((slots, CELLS), 0) == slot_ref[...]).astype(BF16)
    solved = z_ref[...]
    solved = solved + (dot_nn(r_s[1], pick) + dot_nn(r_s[0], pick))
    solved_ref[...] = solved
    top_ref[...] = solved[:, 0:LON]
    bottom_ref[...] = solved[:, CELLS - LON :]
    row = iota((8, CELLS), 0)
    spot = iota((8, CELLS), 1)
    edge = (spot == (row % ROWS) * LON + (row // ROWS) * (LON - 1)).astype(F32)
    edges = dot_nt(edge, solved, HI)
    west_ref[...] = edges[0:ROWS]
    east_ref[...] = edges[ROWS:]


def stencil_kernel(
    solved_ref, north_ref, south_ref, west_ref, east_ref, stencil_ref, *rest, start, count
):
    out_ref, block_s, sems = rest[-3:]
    sides = jnp.transpose(jnp.concatenate([west_ref[...], east_ref[...]], axis=0))
    copies = []
    for part, low in enumerate(range(0, count, CHUNK)):
        size = min(CHUNK, count - low)
        used = slice(low, low + size)
        lane = iota((size, LON), 1)
        rows = [solved_ref[used, r * LON : (r + 1) * LON] for r in range(ROWS)]
        for r in range(ROWS):
            here = rows[r]
            north = north_ref[used, :] if r == 0 else rows[r - 1]
            south = south_ref[used, :] if r == ROWS - 1 else rows[r + 1]
            west = jnp.where(lane == 0, sides[used, r : r + 1], pltpu.roll(here, 1, 1))
            east = jnp.where(
                lane == LON - 1,
                sides[used, ROWS + r : ROWS + r + 1],
                pltpu.roll(here, LON - 1, 1),
            )
            result = here
            for n, side in enumerate((north, south, west, east)):
                coef = stencil_ref[n * ROWS + r : n * ROWS + r + 1, :]
                result = result + coef * (side - here)
            block_s[pl.ds(low * ROWS + r, size, stride=ROWS), :] = result
        copy = pltpu.make_async_copy(
            block_s.at[pl.ds(low * ROWS, size * ROWS), :],
            out_ref.at[pl.ds((start + low) * ROWS, size * ROWS), :],
            sems.at[part],
        )
        copy.start()
        copies.append(copy)
    for copy in copies:
        copy.wait()


def shape_of(*dims, dtype=F32):
    return jax.ShapeDtypeStruct(dims, dtype)


def shift(cells, axis, step):
    count = lax.axis_size(axis)
    pairs = [(i, i + step) for i in range(count) if 0 <= i + step < count]
    return lax.ppermute(cells, axis, pairs)


def on_device(
    fields_in, drag_rate, loss_rate, diffusivity, owner_col, anchor_cell, offsets, stencil
):
    flat_in = fields_in.reshape(FLAT * ROWS, LON)
    request, slot_index = pl.pallas_call(
        request_kernel,
        out_shape=(shape_of(PEERS, LANES), shape_of(1, CELLS, dtype=jnp.int32)),
        name="request",
    )(owner_col.reshape(1, CELLS), anchor_cell.reshape(1, CELLS), offsets)
    got = lax.all_to_all(request, "col", split_axis=0, concat_axis=0, tiled=True)
    rates, inverse = pl.pallas_call(
        inverse_kernel,
        out_shape=(shape_of(LEV_PAD, 8), shape_of(FIELDS, LEV_ROWS, LEV_PAD)),
        scratch_shapes=[
            pltpu.VMEM((8, LEV_PAD), F32),
            pltpu.VMEM((8, LEV_PAD), F32),
            pltpu.VMEM((LEV_PAD * 8, LANES), F32),
            pltpu.VMEM((LEV_PAD * 8, LANES), F32),
        ],
        name="inverse",
    )(drag_rate.reshape(1, LEV), loss_rate, diffusivity)

    def solve(moved):
        return pl.pallas_call(
            partial(solve_kernel, moved=moved),
            out_shape=tuple(shape_of(count, CELLS) for count in COUNTS),
            scratch_shapes=[pltpu.VMEM((FIELDS, LEV_PAD, CELLS), F32)],
            compiler_params=pltpu.CompilerParams(
                vmem_limit_bytes=67_100_000 if moved else 65_000_000
            ),
            name="solve_moved" if moved else "solve_half",
        )(flat_in, rates, inverse)

    sources = solve(True)
    returned = []
    for share, source in zip(SHARES, sources):
        values = pl.pallas_call(
            owner_kernel,
            grid=(PEERS // GROUPS // 2,),
            in_specs=[
                pl.BlockSpec((2 * GROUPS, LANES), lambda i: (i, 0)),
                pl.BlockSpec((GROUPS * share, CELLS), lambda i: (0, 0)),
            ],
            out_specs=pl.BlockSpec((2 * GROUPS, share, LANES), lambda i: (i, 0, 0)),
            out_shape=shape_of(PEERS, share, LANES),
            scratch_shapes=[pltpu.VMEM((GROUPS * share, CELLS), BF16)] * 2,
            name="owner",
        )(got, source)
        returned.append(
            lax.all_to_all(values, "col", split_axis=0, concat_axis=0, tiled=True)
        )
    locals_ = solve(False)
    coefs = stencil.reshape(4 * ROWS, LON)
    out = None
    for start, count, back, local in zip(STARTS, COUNTS, returned, locals_):
        solved, top, bottom, west, east = pl.pallas_call(
            arrive_kernel,
            in_specs=[pl.BlockSpec(memory_space=pl.ANY)]
            + [pl.BlockSpec(memory_space=pltpu.VMEM)] * 2,
            out_shape=(
                shape_of(count, CELLS),
                shape_of(count, LON),
                shape_of(count, LON),
                shape_of(ROWS, count),
                shape_of(ROWS, count),
            ),
            scratch_shapes=[
                pltpu.VMEM((2, count, PEERS * CAP), BF16),
                pltpu.VMEM((PEERS, share, LANES), F32),
                pltpu.SemaphoreType.DMA((PEERS // GROUPS,)),
            ],
            name="arrive",
        )(back, slot_index, local)
        from_north = shift(bottom, "band", 1)
        from_south = shift(top, "band", -1)
        from_west = shift(east, "col", 1)
        from_east = shift(west, "col", -1)
        used = min(count, FLAT - start)
        whole = [] if out is None else [out]
        out = pl.pallas_call(
            partial(stencil_kernel, start=start, count=used),
            out_shape=shape_of(FLAT * ROWS, LON),
            in_specs=[pl.BlockSpec(memory_space=pltpu.VMEM)] * 6
            + [pl.BlockSpec(memory_space=pl.ANY)] * len(whole),
            out_specs=pl.BlockSpec(memory_space=pl.ANY),
            scratch_shapes=[pltpu.VMEM((used * ROWS, LON), F32), pltpu.SemaphoreType.DMA((GROUPS,))],
            input_output_aliases={6: 0} if whole else {},
            name="stencil",
        )(solved, from_north, from_south, from_west, from_east, coefs, *whole)
    return out.reshape(fields_in.shape)


def solution(mesh):
    in_specs = (
        P(None, None, "band", "col"),
        P(),
        P(),
        P(),
        P("band", "col", None),
        P("band", "col"),
        P(None, "band", "col"),
        P(None, "band", "col"),
    )
    out_specs = P(None, None, "band", "col")
    return jax.shard_map(
        on_device, mesh=mesh, in_specs=in_specs, out_specs=out_specs, check_vma=False
    )
```
